32 devices in a mesh: tm: 2 (over x), gx: 4 (over z), gy: 4 (over y, core).
Axes of the slice: x: 2, y: 2, z: 4, core: 2. Of those that a mesh axis runs over, the one named last changes fastest.
Arguments:
- increment: float32 [2, 137, 64, 512], P('tm', None, 'gx', 'gy'), may hold values from -6 to 6
- dual_state: float32 [2, 137, 64, 512], P('tm', None, 'gx', 'gy'), may hold values from -6 to 6
- forcing: float32 [2, 137, 64, 512], P('tm', None, 'gx', 'gy'), may hold values from -6 to 6
- gradient: float32 [2, 137, 64, 512], P('tm', None, 'gx', 'gy'), may hold values from -3 to 3
- courant_x: float32 [2, 137, 64, 512], P('tm', None, 'gx', 'gy'), may hold values from 0.05 to 0.3
- courant_y: float32 [2, 137, 64, 512], P('tm', None, 'gx', 'gy'), may hold values from 0.05 to 0.3
- error_var: float32 [2, 137, 64, 512], P('tm', None, 'gx', 'gy'), may hold values from 0.2 to 2
- obs_weight: float32 [2, 137, 64, 512], P('tm', None, 'gx', 'gy'), may hold values from 0.2 to 2
- diffusion: float32 [137], replicated, may hold values from 0.02 to 0.1
- level_mix: float32 [137, 137], replicated, may hold values from -0.5 to 0.8
Outputs:
- dual_next: float32 [2, 137, 64, 512], P('tm', None, 'gx', 'gy')
- increment_next: float32 [2, 137, 64, 512], P('tm', None, 'gx', 'gy')
The draws below stay inside these ranges and needn't reach their ends.
All inputs are finite; a program needn't handle non-finite values.
Results may differ from the reference program's by a relative error of at most 0.0001.
Values sent between devices are 32-bit elements; how exact they have to be, the bound alone decides.
A program may use at most 128 MiB of HBM per device.

```python
import math
import jax
import jax.numpy as jnp
from jax import lax

LEVELS = 137
STEPS = 3
SUBWIN = 2
NX = 64
NY = 512


def coherent_field(key):
    level_place = ((jnp.arange(LEVELS, dtype=jnp.float32) + 0.5) / LEVELS)[None, :, None, None]
    along_x = (jnp.arange(NX, dtype=jnp.float32) / NX)[None, None, :, None]
    along_y = (jnp.arange(NY, dtype=jnp.float32) / NY)[None, None, None, :]
    window_place = jnp.arange(SUBWIN, dtype=jnp.float32) / max(SUBWIN - 1, 1)
    window_scale = (0.6 + 0.4 * window_place)[:, None, None, None]
    summed = jnp.zeros((SUBWIN, LEVELS, NX, NY), jnp.float32)
    for mode in range(3):
        mode_key = jax.random.fold_in(key, 31 + mode)
        mode_keys = jax.random.split(mode_key, 6)
        wave_x = jax.random.randint(mode_keys[0], (), 1, 3).astype(jnp.float32)
        wave_y = jax.random.randint(mode_keys[1], (), 1, 3).astype(jnp.float32)
        wave_level = jax.random.randint(mode_keys[2], (), 0, 3).astype(jnp.float32)
        phases = jax.random.uniform(mode_keys[3], (3,), jnp.float32, -math.pi, math.pi)
        strength = jax.random.uniform(mode_keys[4], (), jnp.float32, 0.6, 1.0)
        jitter = 1.0 + 0.1 * jax.random.uniform(mode_keys[5], (SUBWIN, 1, 1, 1), jnp.float32, -1.0, 1.0)
        pattern = jnp.cos(2.0 * math.pi * wave_x * along_x + phases[0])
        pattern = pattern * jnp.cos(2.0 * math.pi * wave_y * along_y + phases[1])
        pattern = pattern * jnp.cos(math.pi * wave_level * level_place + phases[2])
        summed = summed + strength * jitter * pattern
    rough_key = jax.random.fold_in(key, 97)
    smooth = 1.4 * summed
    roughness = 0.5 * jnp.clip(jax.random.normal(rough_key, (SUBWIN, LEVELS, NX, NY), jnp.float32), -2.5, 2.5)
    return window_scale * smooth + roughness


def draw_increment(key, part):
    return coherent_field(jax.random.fold_in(key, 101))


def draw_dual_state(key, part):
    return coherent_field(jax.random.fold_in(key, 202))


def draw_forcing(key, part):
    normal_part = 0.5 * jnp.clip(jax.random.normal(key, (SUBWIN, LEVELS, NX, NY), jnp.float32), -4.0, 4.0)
    growth = 1.0 + 2.0 * jnp.arange(SUBWIN, dtype=jnp.float32) / max(SUBWIN - 1, 1)
    growth = growth[:, None, None, None]
    return normal_part * growth


def draw_level_mix(key, part):
    key_diag = jax.random.fold_in(key, 11)
    key_coupling = jax.random.fold_in(key, 23)
    diagonal = jax.random.uniform(key_diag, (LEVELS,), jnp.float32, 0.5, 0.8)
    coupling = jnp.clip(jax.random.normal(key_coupling, (LEVELS, LEVELS), jnp.float32), -6.0, 6.0) * (0.3 / math.sqrt(LEVELS))
    coupling = coupling * (1.0 - jnp.eye(LEVELS, dtype=jnp.float32))
    return coupling + jnp.diag(diagonal)


def block_levels(key, shape, cuts, least, high):
    loudness, own = 1.0, jax.random.fold_in(key, 6)
    for position, blocks in cuts:
        draws = jnp.exp(jax.random.uniform(jax.random.fold_in(own, position), (blocks,), jnp.float32, least / len(cuts), high / len(cuts)))
        loudness = loudness * jnp.repeat(draws, shape[position] // blocks).reshape([-1 if axis == position else 1 for axis in range(len(shape))])
    return loudness


def bell_draw(stream_key, dims, width, limit, cuts=(), kind=jnp.bfloat16):
    entries = jax.random.normal(stream_key, dims, jnp.float32) * width
    if len(cuts) > 0:
        entries = block_levels(stream_key, dims, cuts, -0.22, 0.18) * entries
    return jnp.clip(entries, min=-limit, max=limit).astype(kind)


def setup_inputs(seed: int = 0) -> dict:
    arg_keys = jax.random.split(jax.random.key(seed), 11)
    increment = draw_increment(jax.random.fold_in(arg_keys[10], 71), 0)
    dual_state = draw_dual_state(jax.random.fold_in(arg_keys[10], 71), 0)
    forcing = draw_forcing(jax.random.fold_in(arg_keys[10], 71), 0)
    gradient = bell_draw(arg_keys[3], (SUBWIN, LEVELS, NX, NY), 0.5, 3.0, ((0, 2), (2, 4), (3, 4)), jnp.float32)
    courant_x = jnp.clip(0.05 + 0.25 * jax.random.uniform(arg_keys[4], (SUBWIN, LEVELS, NX, NY), jnp.float32) ** block_levels(arg_keys[4], (SUBWIN, LEVELS, NX, NY), ((0, 2), (2, 4), (3, 4)), -0.2, 0.2), 0.05, 0.3)
    courant_y = jnp.clip(0.05 + 0.25 * jax.random.uniform(arg_keys[5], (SUBWIN, LEVELS, NX, NY), jnp.float32) ** block_levels(arg_keys[5], (SUBWIN, LEVELS, NX, NY), ((0, 2), (2, 4), (3, 4)), -0.2, 0.2), 0.05, 0.3)
    error_var = jnp.clip(jnp.exp(math.log(2.0) - 2.3025851 * jax.random.uniform(arg_keys[6], (SUBWIN, LEVELS, NX, NY), jnp.float32) ** block_levels(arg_keys[6], (SUBWIN, LEVELS, NX, NY), ((0, 2), (2, 4), (3, 4)), -0.2, 0.2)), 0.2, 2.0)
    obs_weight = jnp.clip(jnp.exp(math.log(2.0) - 2.3025851 * jax.random.uniform(arg_keys[7], (SUBWIN, LEVELS, NX, NY), jnp.float32) ** block_levels(arg_keys[7], (SUBWIN, LEVELS, NX, NY), ((0, 2), (2, 4), (3, 4)), -0.2, 0.2)), 0.2, 2.0)
    diffusion = jnp.clip(jnp.exp(jax.random.uniform(arg_keys[8], (LEVELS,), jnp.float32, math.log(0.02), math.log(0.1))), 0.02, 0.1)
    level_mix = draw_level_mix(jax.random.fold_in(arg_keys[10], 71), 0)
    return dict(increment=increment, dual_state=dual_state, forcing=forcing, gradient=gradient, courant_x=courant_x, courant_y=courant_y, error_var=error_var, obs_weight=obs_weight, diffusion=diffusion, level_mix=level_mix)


def apply_levels(matrix, current):
    return jnp.einsum('lm,mxy->lxy', matrix, current, precision=lax.Precision.HIGHEST)

def neighbours(current):
    padded = jnp.pad(current, ((0, 0), (1, 1), (1, 1)))
    return (padded[:, :-2, 1:-1], padded[:, 2:, 1:-1], padded[:, 1:-1, :-2], padded[:, 1:-1, 2:])

def tangent_step(current, courant_x, courant_y, lower_x, lower_y, spread, level_mix):
    minus_x, plus_x, minus_y, plus_y = neighbours(current)
    advected = (1.0 - courant_x - courant_y - 4.0 * spread) * current + lower_x * minus_x + lower_y * minus_y
    advected = advected + spread * (minus_x + plus_x + minus_y + plus_y)
    return apply_levels(level_mix, advected)

def adjoint_step(current, courant_x, courant_y, spread, level_mix):
    mixed_back = apply_levels(level_mix.T, current)
    minus_x, plus_x, minus_y, plus_y = neighbours(mixed_back)
    result = (1.0 - courant_x - courant_y - 4.0 * spread) * mixed_back + courant_x * plus_x + courant_y * plus_y
    return result + spread * (minus_x + plus_x + minus_y + plus_y)

def reference(increment, dual_state, forcing, gradient, courant_x, courant_y, error_var, obs_weight, diffusion, level_mix):
    spread = diffusion[:, None, None]
    windows = increment.shape[0]
    end_states = []
    back_states = []
    for window in range(windows):
        flow_x = courant_x[window]
        flow_y = courant_y[window]
        lower_x = jnp.pad(flow_x, ((0, 0), (1, 0), (0, 0)))[:, :-1, :]
        lower_y = jnp.pad(flow_y, ((0, 0), (0, 0), (1, 0)))[:, :, :-1]
        forward_state = increment[window]
        for substep in range(STEPS):
            forward_state = tangent_step(forward_state, flow_x, flow_y, lower_x, lower_y, spread, level_mix)
        end_states.append(forward_state)
        if window + 1 < windows:
            adjoint_state = dual_state[window + 1]
        else:
            adjoint_state = jnp.zeros_like(dual_state[0])
        for substep in range(STEPS):
            adjoint_state = adjoint_step(adjoint_state, flow_x, flow_y, spread, level_mix)
        back_states.append(adjoint_state)
    earlier_end = jnp.stack([jnp.zeros_like(increment[0])] + end_states[:-1])
    back_all = jnp.stack(back_states)
    residual_dual = forcing - error_var * dual_state - increment + earlier_end
    residual_incr = gradient - obs_weight * increment - dual_state + back_all
    global_sum = jnp.sum(residual_dual * residual_dual) + jnp.sum(residual_incr * residual_incr)
    cell_count = 2 * residual_dual.size
    root_mean = jnp.sqrt(global_sum / cell_count + 1e-06)
    step_scale = jnp.minimum(1.0, 0.5 / root_mean)
    return (dual_state + step_scale * residual_dual, increment + step_scale * residual_incr)
```

```python
import functools

import jax
import jax.numpy as jnp
from jax import lax
from jax.experimental import pallas as pl
from jax.experimental.pallas import tpu as pltpu
from jax.sharding import PartitionSpec as P

STEPS = 3


def shifted(block, axis, distance):
    devices = range(lax.axis_size(axis))
    route = [(i - distance, i) for i in devices if i - distance in devices]
    return lax.ppermute(block, axis, route)


def summed(value, axis):
    count = lax.axis_size(axis)
    if count & (count - 1):
        return lax.psum(value, axis)
    bit = 1
    while bit < count:
        value = value + lax.ppermute(value, axis, [(i, i ^ bit) for i in range(count)])
        bit *= 2
    return value


def split(block):
    high = block.astype(jnp.bfloat16)
    return high, (block - high.astype(jnp.float32)).astype(jnp.bfloat16)


def mixed(high, low, block):
    block_high, block_low = split(block)
    dot = functools.partial(jnp.dot, preferred_element_type=jnp.float32)
    return dot(high, block_low) + dot(low, block_high) + dot(high, block_high)


def kernel(
    adjoint, stencil, mix, v, x_low, x_high, y_low, y_high, a, b, a_low, b_low, s, matrix, out
):
    rows, levels, width = v.shape
    high, low = split(matrix[...])
    lane = lax.broadcasted_iota(jnp.int32, (levels, width), 1)

    def row(i):
        current = v[i]
        if not stencil:
            return current
        spread = s[...]
        minus_x = v[i - 1] if i else x_low[0]
        plus_x = v[i + 1] if i < rows - 1 else x_high[0]
        minus_y = jnp.where(lane == 0, y_low[i], pltpu.roll(current, 1, 1))
        plus_y = jnp.where(lane == width - 1, y_high[i], pltpu.roll(current, width - 1, 1))
        flow_x, flow_y = a[i], b[i]
        result = (1.0 - flow_x - flow_y - 4.0 * spread) * current
        if adjoint:
            result = result + flow_x * plus_x + flow_y * plus_y
        else:
            lower_x = a[i - 1] if i else a_low[0]
            lower_y = jnp.where(lane == 0, b_low[i], pltpu.roll(flow_y, 1, 1))
            result = result + lower_x * minus_x + lower_y * minus_y
        return result + spread * (minus_x + plus_x + minus_y + plus_y)

    group = 2 if rows % 2 == 0 else 1
    for i in range(0, rows, group):
        parts = [row(i + k) for k in range(group)]
        if mix:
            block = jnp.concatenate(parts, axis=1) if group > 1 else parts[0]
            result = mixed(high, low, block)
            parts = [result[:, k * width : (k + 1) * width] for k in range(group)]
        for k in range(group):
            out[i + k] = parts[k]


def step(adjoint, stencil, mix, *operands):
    state = operands[0]
    flops = 2 * 3 * state.size * state.shape[1]
    return pl.pallas_call(
        functools.partial(kernel, adjoint, stencil, mix),
        out_shape=jax.ShapeDtypeStruct(state.shape, state.dtype),
        in_specs=[pl.BlockSpec(memory_space=pltpu.VMEM)] * len(operands),
        out_specs=pl.BlockSpec(memory_space=pltpu.VMEM),
        compiler_params=pltpu.CompilerParams(vmem_limit_bytes=40 * 1024 * 1024),
        cost_estimate=pl.CostEstimate(
            flops=flops, bytes_accessed=16 * state.size, transcendentals=0
        ),
    )(*operands)


def rims(state):
    x_low = shifted(state[-1:], "gx", 1)
    x_high = shifted(state[:1], "gx", -1)
    y_low = shifted(state[:, :, -1], "gy", 1)[:, :, None]
    y_high = shifted(state[:, :, 0], "gy", -1)[:, :, None]
    return x_low, x_high, y_low, y_high


def local(
    increment,
    dual_state,
    forcing,
    gradient,
    courant_x,
    courant_y,
    error_var,
    obs_weight,
    diffusion,
    level_mix,
):
    initial = increment[0]
    dual_now = dual_state[0]
    later = shifted(dual_now, "tm", -1)
    forward, backward, flow_x, flow_y = (
        jnp.swapaxes(part, 0, 1) for part in (initial, later, courant_x[0], courant_y[0])
    )
    a_low = shifted(flow_x[-1:], "gx", 1)
    b_low = shifted(flow_y[:, :, -1], "gy", 1)[:, :, None]
    flows = (flow_x, flow_y, a_low, b_low, diffusion[:, None])
    back = level_mix.T
    zeros = tuple(jnp.zeros_like(part) for part in (a_low, a_low, b_low, b_low))
    backward = step(True, False, True, backward, *zeros, *flows, back)
    for substep in range(STEPS):
        forward = step(False, True, True, forward, *rims(forward), *flows, level_mix)
        last = substep == STEPS - 1
        backward = step(True, True, not last, backward, *rims(backward), *flows, back)
    forward_state = jnp.swapaxes(forward, 0, 1)
    adjoint_state = jnp.swapaxes(backward, 0, 1)
    earlier_end = shifted(forward_state, "tm", 1)
    residual_dual = forcing[0] - error_var[0] * dual_now - initial + earlier_end
    residual_incr = gradient[0] - obs_weight[0] * initial - dual_now + adjoint_state
    squares = jnp.sum(residual_dual * residual_dual) + jnp.sum(residual_incr * residual_incr)
    global_sum = squares
    for axis in ("gy", "gx", "tm"):
        global_sum = summed(global_sum, axis)
    cell_count = (
        2 * residual_dual.size * lax.axis_size("tm") * lax.axis_size("gx") * lax.axis_size("gy")
    )
    root_mean = jnp.sqrt(global_sum / cell_count + 1e-06)
    step_scale = jnp.minimum(1.0, 0.5 / root_mean)
    dual_next = dual_now + step_scale * residual_dual
    increment_next = initial + step_scale * residual_incr
    return (dual_next[None], increment_next[None])


def solution(mesh):
    in_specs = (
        P("tm", None, "gx", "gy"),
        P("tm", None, "gx", "gy"),
        P("tm", None, "gx", "gy"),
        P("tm", None, "gx", "gy"),
        P("tm", None, "gx", "gy"),
        P("tm", None, "gx", "gy"),
        P("tm", None, "gx", "gy"),
        P("tm", None, "gx", "gy"),
        P(),
        P(),
    )
    out_specs = (P("tm", None, "gx", "gy"), P("tm", None, "gx", "gy"))
    return jax.shard_map(local, mesh=mesh, in_specs=in_specs, out_specs=out_specs, check_vma=False)
```
